256 devices in a mesh: blk: 128 (over z, x, y), rep: 2 (over core).
Axes of the slice: x: 4, y: 4, z: 8, core: 2. Of those that a mesh axis runs over, the one named last changes fastest.
Arguments:
- hamiltonian: bfloat16 [1024, 7, 128, 128], P(('blk', 'rep')), may hold values from -0.7 to 0.7
- lists: int32 [1024, 4], P(('blk', 'rep')), may hold values from 0 to 1023, as said below
- scales: float32 [1024], P(('blk', 'rep')), may hold values from 0.8 to 1.2
- weights: float32 [1024, 4], P(('blk', 'rep')), may hold values from 0.25 to 1
Outputs:
- density: float32 [1024, 7, 128, 128], P(('blk', 'rep'))
The draws below stay inside these ranges and needn't reach their ends.
Inputs may be any that keep to these rules, and one draw needn't show every extreme that they name: lists[j, 0] is j; the other entries of a row are distinct, differ from j, and lie within 3 blocks of j counted modulo 1024.
All inputs are finite; a program needn't handle non-finite values.
Results may differ from the reference program's by a relative error of at most 0.00096.
Values may be sent and summed in bfloat16 or wider, within the bound.
A program may use at most 64 MiB of HBM per device.

```python
import math
import jax
import jax.numpy as jnp
from jax import lax

B = 128
LIST = 4
W = 3
REACH = 3
ITERS = 5
BAND = 7
NB = 1024


def draw_hamiltonian(key, part):
    noise_key, onsite_key = jax.random.split(jax.random.fold_in(key, 11), 2)
    blocks = 0.012 * jax.random.truncated_normal(noise_key, -4.0, 4.0, (NB, BAND, B, B), jnp.float32)
    onsite = jax.random.uniform(onsite_key, (NB, B), jnp.float32, -0.6, 0.6)
    identity = jnp.eye(B, dtype=jnp.float32)
    centre = (jnp.arange(BAND) == W).astype(jnp.float32)
    blocks = blocks + onsite[:, None, :, None] * identity[None, None, :, :] * centre[None, :, None, None]
    return blocks.astype(jnp.bfloat16)


def draw_lists(key, part):
    offsets = jnp.concatenate([jnp.arange(-REACH, 0), jnp.arange(1, REACH + 1)]).astype(jnp.int32)
    scores = jax.random.randint(jax.random.fold_in(key, 23), (NB, 2 * REACH), 0, 1 << 20) * (2 * REACH)
    scores = scores + jnp.arange(2 * REACH, dtype=jnp.int32)[None, :]
    order = jnp.argsort(scores, axis=1, stable=True)
    picked = offsets[order[:, :LIST - 1]]
    centre = jnp.arange(NB, dtype=jnp.int32)[:, None]
    return jnp.concatenate([centre, (centre + picked) % NB], axis=1).astype(jnp.int32)


def steps_of(rng, extent, shards, least, largest):
    level = 1.0
    for position, blocks in shards:
        heights = jax.random.uniform(jax.random.fold_in(jax.random.fold_in(rng, 6), position), (blocks,), jnp.float32, least / len(shards), largest / len(shards))
        level = level * jnp.repeat(jnp.exp(heights), extent[position] // blocks).reshape((-1,) + (1,) * (len(extent) - 1 - position))
    return level


def setup_inputs(seed: int = 0) -> dict:
    key_list = jax.random.split(jax.random.key(seed), 5)
    hamiltonian = draw_hamiltonian(jax.random.fold_in(key_list[4], 71), 0)
    lists = draw_lists(jax.random.fold_in(key_list[4], 71), 0)
    scales = jnp.clip(jnp.exp(math.log(1.2) - 0.40546513 * jax.random.uniform(key_list[2], (NB,), jnp.float32) ** steps_of(key_list[2], (NB,), ((0, 256),), -0.2, 0.2)), 0.8, 1.2)
    weights = jnp.clip(0.25 + 0.75 * jax.random.uniform(key_list[3], (NB, LIST), jnp.float32) ** steps_of(key_list[3], (NB, LIST), ((0, 256),), -0.2, 0.2), 0.25, 1.0)
    return {"hamiltonian": hamiltonian, "lists": lists, "scales": scales, "weights": weights}


def wrapped(delta, total):
    half_total = total // 2
    return (delta + half_total) % total - half_total


def assemble(blocks, valid):
    upper = jnp.where(valid[:, :, None, None], blocks.astype(jnp.float32), jnp.float32(0.0))
    both = 0.5 * (upper + jnp.transpose(upper, (1, 0, 3, 2)))
    count, width = both.shape[0], both.shape[2]
    return jnp.transpose(both, (0, 2, 1, 3)).reshape(count * width, count * width)


def sign_density(matrix, scale):
    current = scale * matrix
    for step in range(ITERS):
        rounded = current.astype(jnp.bfloat16)
        square = jnp.dot(rounded, rounded, preferred_element_type=jnp.float32).astype(jnp.bfloat16)
        current = 1.5 * current - 0.5 * jnp.dot(rounded, square, preferred_element_type=jnp.float32)
    order = matrix.shape[0]
    return 0.5 * (jnp.eye(order, dtype=jnp.float32) - current)


def reference(hamiltonian, lists, scales, weights):
    total, band, width = hamiltonian.shape[0], hamiltonian.shape[1], hamiltonian.shape[2]
    half_band = band // 2

    def visit(accum, inputs):
        members, scale, share = inputs
        members = members.astype(jnp.int32)
        offset = wrapped(members[None, :] - members[:, None], total).astype(jnp.int32)
        valid = jnp.abs(offset) <= half_band
        slot = jnp.clip(offset + half_band, 0, band - 1).astype(jnp.int32)
        blocks = hamiltonian[members[:, None], slot]
        density = sign_density(assemble(blocks, valid), scale)
        count = members.shape[0]
        pieces = jnp.transpose(density.reshape(count, width, count, width), (0, 2, 1, 3))
        pieces = jnp.where(valid[:, :, None, None], pieces * share[:, None, None, None], jnp.float32(0.0))
        accum = accum.at[members[:, None], slot].add(pieces)
        return accum, None

    accum = jnp.zeros(hamiltonian.shape, jnp.float32)
    accum, unused = lax.scan(visit, accum, (lists, scales, weights))
    return accum
```

```python
import jax
import jax.numpy as jnp
from jax import lax
from jax.experimental import pallas as pl
from jax.experimental.pallas import tpu as pltpu
from jax.sharding import PartitionSpec as P

B = 128
LIST = 4
W = 3
ITERS = 5
BAND = 7
ROWS = 4
EXT = ROWS + 2 * W
F32 = jnp.float32
BF16 = jnp.bfloat16
MESH = pl.DeviceIdType.MESH


def terms(row, col):
    low, high = min(row, col), max(row, col)
    return [z for z in range(ROWS) if z <= low and high <= z + 2 * W]


FAR = [(r, c) for r in range(W) for c in range(r + W + 1)]
NEAR = [(9 - r, 9 - c) for r, c in FAR]
FAR_SENDS = [[t for t in FAR if max(terms(*t)) == z] for z in range(W)]
NEAR_SENDS = [
    [t for t in NEAR if terms(*t) == [ROWS - 1]],
    [t for t in NEAR if terms(*t) != [ROWS - 1]],
]
STARTS = [0, 6, 11]
FAR_ORDER = sum(FAR_SENDS, [])
NEAR_ORDER = sum(NEAR_SENDS, [])


def kernel(
    lists, weights, scales, ham, owned, window, sym, xs, ys, qs, result,
    far_out, near_out, far_in, near_in,
    load_sem, halo_send, halo_recv, far_send, far_recv, near_send, near_recv,
):
    chip = lax.axis_index("blk")
    core = lax.axis_index("rep")
    chips = lax.axis_size("blk")
    total = ROWS * 2 * chips
    first = (chip * 2 + core) * ROWS
    near = (chip, 1 - core)
    far = (lax.rem(chip + 2 * core - 1 + chips, chips), 1 - core)

    def mirrored(value, last):
        return value + core * (last - 2 * value)

    load = pltpu.make_async_copy(ham, window.at[pl.ds(W, ROWS)], load_sem)
    load.start()
    barrier = pltpu.get_barrier_semaphore()
    for device in (near, far):
        pl.semaphore_signal(barrier, inc=1, device_id=device, device_id_type=MESH)

    position, place, share, member = [], [], [], []
    for z in range(ROWS):
        j = mirrored(z, ROWS - 1)
        spots = []
        for a in range(LIST):
            e = jnp.clip(lax.rem(lists[j, a] - first + W + total, total), 0, EXT - 1)
            spots.append(mirrored(e, EXT - 1))
        position.append(spots)
        places, shares, members = [], [], []
        for u in range(2 * W + 1):
            where = jnp.int32(0)
            weight = jnp.float32(0.0)
            here = jnp.float32(0.0)
            for a in range(LIST):
                hit = spots[a] == z + u
                where = jnp.where(hit, jnp.int32(a), where)
                weight = jnp.where(hit, weights[j, a], weight)
                here = jnp.where(hit, jnp.float32(1.0), here)
            places.append(where)
            shares.append(weight)
            members.append(here)
        place.append(places)
        share.append(shares)
        member.append(members)

    pl.semaphore_wait(barrier, 2)

    def halo(side, device, index):
        copies, arrivals = [], []
        for d in (1, 2, 3):
            count = BAND - d
            row = (1 - side) * (d - 1) + side * (ROWS - d)
            there = (1 - side) * (EXT - 1 - W + d) + side * (W - d)
            here = side * (EXT - 1 - W + d) + (1 - side) * (W - d)
            low = side * d
            low_here = (1 - side) * d
            copies.append(pltpu.make_async_remote_copy(
                src_ref=ham.at[row, pl.ds(low, count)],
                dst_ref=window.at[there, pl.ds(low, count)],
                send_sem=halo_send.at[index, d - 1],
                recv_sem=halo_recv.at[index, d - 1],
                device_id=device,
                device_id_type=MESH,
            ))
            arrivals.append(pltpu.make_async_remote_copy(
                src_ref=ham.at[row, pl.ds(low, count)],
                dst_ref=window.at[here, pl.ds(low_here, count)],
                send_sem=halo_send.at[index, d - 1],
                recv_sem=halo_recv.at[index, d - 1],
                device_id=device,
                device_id_type=MESH,
            ))
        return copies, arrivals

    far_copies, far_arrivals = halo(core, far, 0)
    near_copies, near_arrivals = halo(1 - core, near, 1)
    for d in range(W):
        near_copies[d].start()
        far_copies[d].start()

    def symmetrize(low, o):
        high = low + o
        slot = W + o * (1 - 2 * core)
        upper = window[mirrored(low, EXT - 1), slot]
        lower = window[mirrored(high, EXT - 1), 2 * W - slot]
        both = 0.5 * (upper.astype(F32) + lower.T.astype(F32))
        sym[low, W + o] = both
        if o:
            sym[high, W - o] = 0.5 * (lower.astype(F32) + upper.T.astype(F32))

    load.wait()
    for o in range(W + 1):
        for low in range(W, W + ROWS - o):
            symmetrize(low, o)
    for arrival in near_arrivals:
        arrival.wait_recv()
    for o in range(W + 1):
        for high in range(W + ROWS, EXT):
            symmetrize(high - o, o)

    diagonal = (
        lax.broadcasted_iota(jnp.int32, (B, B), 0) == lax.broadcasted_iota(jnp.int32, (B, B), 1)
    ).astype(F32)

    def assemble(z):
        j = mirrored(z, ROWS - 1)
        scale = scales[j]
        spots = []
        for a in range(LIST):
            e = jnp.clip(lax.rem(lists[j, a] - first + W + total, total), 0, EXT - 1)
            spots.append(mirrored(e, EXT - 1))
        for a in range(LIST):
            for b in range(LIST):
                offset = spots[b] - spots[a]
                stored = jnp.where(jnp.abs(offset) <= W, scale, jnp.float32(0.0))
                slot = jnp.clip(offset + W, 0, BAND - 1)
                block = stored * sym[spots[a], slot]
                xs[a * B : a * B + B, b * B : b * B + B] = block
                ys[0, a * B : a * B + B, b * B : b * B + B] = block.astype(BF16)

    def iterate(z):
        half = LIST * B // 2
        for k in range(ITERS):
            now, later = k % 2, (k + 1) % 2
            for m in range(0, LIST * B, half):
                qs[now, m : m + half, :] = jnp.dot(
                    ys[now, m : m + half, :], ys[now], preferred_element_type=F32
                ).astype(BF16)
            for m in range(0, LIST * B, half):
                value = 1.5 * xs[m : m + half, :] - 0.5 * jnp.dot(
                    ys[now, m : m + half, :], qs[now], preferred_element_type=F32
                )
                if k < ITERS - 1:
                    xs[m : m + half, :] = value
                    ys[later, m : m + half, :] = value.astype(BF16)
                    continue
                for a in range(m // B, (m + half) // B):
                    for b in range(LIST):
                        block = value[a * B - m : a * B - m + B, b * B : b * B + B]
                        if a == b:
                            result[z * LIST * LIST + a * LIST + b] = 0.5 * (diagonal - block)
                        else:
                            result[z * LIST * LIST + a * LIST + b] = -0.5 * block

    def gathered(row, col):
        value = None
        for z in terms(row, col):
            u, v = row - z, col - z
            factor = share[z][u] * member[z][v]
            term = factor * result[z * LIST * LIST + place[z][u] * LIST + place[z][v]]
            value = term if value is None else value + term
        return value

    def contribution(z):
        low, count = STARTS[z], len(FAR_SENDS[z])
        return pltpu.make_async_remote_copy(
            src_ref=far_out.at[pl.ds(low, count)],
            dst_ref=far_in.at[pl.ds(low, count)],
            send_sem=far_send.at[z],
            recv_sem=far_recv.at[z],
            device_id=far,
            device_id_type=MESH,
        )

    def near_contribution(i):
        low, count = i * len(NEAR_SENDS[0]), len(NEAR_SENDS[i])
        return pltpu.make_async_remote_copy(
            src_ref=near_out.at[pl.ds(low, count)],
            dst_ref=near_in.at[pl.ds(low, count)],
            send_sem=near_send.at[i],
            recv_sem=near_recv.at[i],
            device_id=near,
            device_id_type=MESH,
        )

    def send_far(z):
        for i, target in enumerate(FAR_SENDS[z]):
            far_out[STARTS[z] + i] = gathered(*target)
        contribution(z).start()

    def send_near(i):
        for n, target in enumerate(NEAR_SENDS[i]):
            near_out[i * len(NEAR_SENDS[0]) + n] = gathered(*target)
        near_contribution(i).start()

    def step(t, carry):
        z = lax.rem(t + ROWS - 1, ROWS)

        @pl.when(t == 1)
        def _():
            for arrival in far_arrivals:
                arrival.wait_recv()
            for o in range(W + 1):
                for low in range(W):
                    symmetrize(low, o)

        assemble(z)
        iterate(z)

        @pl.when(t == 0)
        def _():
            send_near(0)

        for sent in range(W):
            @pl.when(t == sent + 1)
            def _():
                send_far(sent)

        return carry

    lax.fori_loop(0, ROWS, step, 0)
    send_near(1)

    def spot(row, col):
        return mirrored(row - W, ROWS - 1), mirrored(col - row + W, BAND - 1)

    for row in range(W, W + ROWS):
        for col in range(row - W, row + W + 1):
            r, s = spot(row, col)
            owned[r, s] = gathered(row, col)

    def add_far(z):
        contribution(z).wait_recv()
        for i, (row, col) in enumerate(FAR_SENDS[z]):
            r, s = spot(5 - row, 5 - col)
            owned[r, s] += far_in[STARTS[z] + i]

    def add_near(i):
        near_contribution(i).wait_recv()
        for n, (row, col) in enumerate(NEAR_SENDS[i]):
            r, s = spot(13 - row, 13 - col)
            owned[r, s] += near_in[i * len(NEAR_SENDS[0]) + n]

    add_near(0)
    add_far(0)
    add_far(1)
    add_near(1)
    add_far(2)
    for d in range(W):
        near_copies[d].wait_send()
        far_copies[d].wait_send()
    for z in range(W):
        contribution(z).wait_send()
    for i in range(2):
        near_contribution(i).wait_send()


def on_device(hamiltonian, lists, scales, weights):
    smem = pl.BlockSpec(memory_space=pltpu.SMEM)
    hbm = pl.BlockSpec(memory_space=pl.ANY)
    operands = [
        pltpu.with_memory_space_constraint(value, pltpu.HBM)
        for value in (lists, weights, scales, hamiltonian)
    ]
    size = LIST * B
    return pl.pallas_call(
        kernel,
        name="density",
        out_shape=jax.ShapeDtypeStruct((ROWS, BAND, B, B), F32),
        in_specs=[smem, smem, smem, hbm],
        out_specs=pl.BlockSpec(memory_space=pltpu.VMEM),
        scratch_shapes=[
            pltpu.VMEM((EXT, BAND, B, B), BF16),
            pltpu.VMEM((EXT, BAND, B, B), F32),
            pltpu.VMEM((size, size), F32),
            pltpu.VMEM((2, size, size), BF16),
            pltpu.VMEM((2, size, size), BF16),
            pltpu.VMEM((ROWS * LIST * LIST, B, B), F32),
            pltpu.VMEM((len(FAR), B, B), F32),
            pltpu.VMEM((len(NEAR), B, B), F32),
            pltpu.VMEM((len(FAR), B, B), F32),
            pltpu.VMEM((len(NEAR), B, B), F32),
            pltpu.SemaphoreType.DMA,
            pltpu.SemaphoreType.DMA((2, W)),
            pltpu.SemaphoreType.DMA((2, W)),
            pltpu.SemaphoreType.DMA((W,)),
            pltpu.SemaphoreType.DMA((W,)),
            pltpu.SemaphoreType.DMA((2,)),
            pltpu.SemaphoreType.DMA((2,)),
        ],
        compiler_params=pltpu.CompilerParams(
            collective_id=0, has_side_effects=True, vmem_limit_bytes=40 << 20
        ),
    )(*operands)


def solution(mesh):
    in_specs = (
        P(("blk", "rep"), None, None, None),
        P(("blk", "rep"), None),
        P(("blk", "rep")),
        P(("blk", "rep"), None),
    )
    out_specs = P(("blk", "rep"), None, None, None)
    return jax.shard_map(
        on_device, mesh=mesh, in_specs=in_specs, out_specs=out_specs, check_vma=False
    )
```

```python
import jax
import jax.numpy as jnp
from jax import lax
from jax.experimental import pallas as pl
from jax.experimental.pallas import tpu as pltpu
from jax.sharding import PartitionSpec as P

B = 128
LIST = 4
W = 3
ITERS = 5
BAND = 7
ROWS = 4
EXT = ROWS + 2 * W
F32 = jnp.float32
BF16 = jnp.bfloat16
MESH = pl.DeviceIdType.MESH


def terms(row, col):
    low, high = min(row, col), max(row, col)
    return [z for z in range(ROWS) if z <= low and high <= z + 2 * W]


FAR = [(r, c) for r in range(W) for c in range(r + W + 1)]
NEAR = [(9 - r, 9 - c) for r, c in FAR]
FAR_SENDS = [[t for t in FAR if max(terms(*t)) == z] for z in range(W)]
NEAR_SENDS = [
    [t for t in NEAR if terms(*t) == [ROWS - 1]],
    [t for t in NEAR if terms(*t) != [ROWS - 1]],
]
STARTS = [0, 6, 11]
EARLY = 3


def kernel(
    lists_hbm, weights_hbm, scales_hbm, ham, owned, lists, weights, scales, window, sym, xs, ys, qs, result,
    far_out, far_line_out, near_out, far_in, far_line_in, near_in,
    small_sem, load_sem, halo_send, halo_recv, far_send, far_recv, near_send, near_recv,
):
    chip = lax.axis_index("blk")
    core = lax.axis_index("rep")
    chips = lax.axis_size("blk")
    total = ROWS * 2 * chips
    first = (chip * 2 + core) * ROWS
    near = (chip, 1 - core)
    far = (lax.rem(chip + 2 * core - 1 + chips, chips), 1 - core)

    def mirrored(value, last):
        return value + core * (last - 2 * value)

    barrier = pltpu.get_barrier_semaphore()
    for device in (far, near):
        pl.semaphore_signal(barrier, inc=1, device_id=device, device_id_type=MESH)
    small = [
        pltpu.make_async_copy(source, target, small_sem.at[i])
        for i, (source, target) in enumerate(
            ((lists_hbm, lists), (weights_hbm, weights), (scales_hbm, scales))
        )
    ]
    for copy in small:
        copy.start()
    load = pltpu.make_async_copy(ham, window.at[pl.ds(W, ROWS)], load_sem)
    load.start()
    for copy in small:
        copy.wait()

    position, place, share, member = [], [], [], []
    for z in range(ROWS):
        j = mirrored(z, ROWS - 1)
        spots = []
        for a in range(LIST):
            e = jnp.clip(lax.rem(lists[j, a] - first + W + total, total), 0, EXT - 1)
            spots.append(mirrored(e, EXT - 1))
        position.append(spots)
        places, shares, members = [], [], []
        for u in range(2 * W + 1):
            where = jnp.int32(0)
            weight = jnp.float32(0.0)
            here = jnp.float32(0.0)
            for a in range(LIST):
                hit = spots[a] == z + u
                where = jnp.where(hit, jnp.int32(a), where)
                weight = jnp.where(hit, weights[j, a], weight)
                here = jnp.where(hit, jnp.float32(1.0), here)
            places.append(where)
            shares.append(weight)
            members.append(here)
        place.append(places)
        share.append(shares)
        member.append(members)

    pl.semaphore_wait(barrier, 2)

    far_runs = [[(2, 3, 4)], [(1, 3, 4), (2, 2, 1)], [(0, 3, 4), (1, 2, 1), (2, 1, 1)]]
    near_runs = [[(7, 0, 6), (8, 0, 5), (9, 0, 4)]]

    def halo(runs, device, corner, index):
        copies, arrivals = [], []
        for y, slot, count in runs:
            flipped = BAND - slot - count
            low = core * slot + (1 - core) * flipped
            low_here = (1 - core) * slot + core * flipped
            row = mirrored(corner - y, EXT - 1) - W
            there = core * y + (1 - core) * (EXT - 1 - y)
            for dst, source, kept in ((there, low, copies), (mirrored(y, EXT - 1), low_here, arrivals)):
                kept.append(pltpu.make_async_remote_copy(
                    src_ref=ham.at[row, pl.ds(source, count)],
                    dst_ref=window.at[dst, pl.ds(source, count)],
                    send_sem=halo_send.at[index],
                    recv_sem=halo_recv.at[index],
                    device_id=device,
                    device_id_type=MESH,
                ))
            index += 1
        return copies, arrivals

    near_copies, near_arrivals = halo(near_runs[0], near, 13, 0)
    far_copies, far_arrivals = [], []
    index = 3
    for runs in far_runs:
        copies, arrivals = halo(runs, far, 5, index)
        far_copies.append(copies)
        far_arrivals.append(arrivals)
        index += len(runs)
    for copy in near_copies + sum(far_copies, []):
        copy.start()

    def symmetrize(low, o):
        high = low + o
        slot = W + o * (1 - 2 * core)
        upper = window[mirrored(low, EXT - 1), slot]
        lower = window[mirrored(high, EXT - 1), 2 * W - slot]
        both = 0.5 * (upper.astype(F32) + lower.T.astype(F32))
        sym[low, W + o] = both
        if o:
            sym[high, W - o] = 0.5 * (lower.astype(F32) + upper.T.astype(F32))

    load.wait()
    for o in range(W + 1):
        for low in range(W, W + ROWS - o):
            symmetrize(low, o)
    for arrival in near_arrivals:
        arrival.wait_recv()
    for o in range(W + 1):
        for high in range(W + ROWS, EXT):
            symmetrize(high - o, o)

    on_diagonal = (
        lax.broadcasted_iota(jnp.int32, (B, B), 0) == lax.broadcasted_iota(jnp.int32, (B, B), 1)
    )
    diagonal = on_diagonal.astype(F32)
    size, half = LIST * B, LIST * B // 2

    def assemble(z):
        spots = position[z]
        scale = scales[mirrored(z, ROWS - 1)]
        for a in range(LIST):
            for b in range(LIST):
                offset = spots[b] - spots[a]
                stored = jnp.where(jnp.abs(offset) <= W, scale, jnp.float32(0.0))
                slot = jnp.clip(offset + W, 0, BAND - 1)
                block = stored * sym[spots[a], slot]
                xs[z, a * B : a * B + B, b * B : b * B + B] = block
                ys[z, 0, a * B : a * B + B, b * B : b * B + B] = block.astype(BF16)

    def iterate(z, steps):
        for k in steps:
            now, later = k % 2, (k + 1) % 2
            for m in range(0, size, half):
                qs[z, now, m : m + half, :] = jnp.dot(
                    ys[z, now, m : m + half, :], ys[z, now], preferred_element_type=F32
                ).astype(BF16)
            for m in range(0, size, half):
                value = 1.5 * xs[z, m : m + half, :] - 0.5 * jnp.dot(
                    ys[z, now, m : m + half, :], qs[z, now], preferred_element_type=F32
                )
                if k < ITERS - 1:
                    xs[z, m : m + half, :] = value
                    ys[z, later, m : m + half, :] = value.astype(BF16)
                    continue
                for a in range(m // B, (m + half) // B):
                    for b in range(LIST):
                        block = value[a * B - m : a * B - m + B, b * B : b * B + B]
                        if a == b:
                            result[z * LIST * LIST + a * LIST + b] = 0.5 * (diagonal - block)
                        else:
                            result[z * LIST * LIST + a * LIST + b] = -0.5 * block

    def gathered(row, col):
        value = None
        for z in terms(row, col):
            u, v = row - z, col - z
            factor = share[z][u] * member[z][v]
            term = factor * result[z * LIST * LIST + place[z][u] * LIST + place[z][v]]
            value = term if value is None else value + term
        return value

    def far_contributions(z):
        low, count = STARTS[z], len(FAR_SENDS[z])
        return [
            pltpu.make_async_remote_copy(
                src_ref=source,
                dst_ref=target,
                send_sem=far_send.at[z, i],
                recv_sem=far_recv.at[z, i],
                device_id=far,
                device_id_type=MESH,
            )
            for i, (source, target) in enumerate((
                (far_line_out.at[z], far_line_in.at[z]),
                (far_out.at[pl.ds(low, count)], far_in.at[pl.ds(low, count)]),
            ))
        ]

    def near_contribution(i):
        low, count = i * len(NEAR_SENDS[0]), len(NEAR_SENDS[i])
        return pltpu.make_async_remote_copy(
            src_ref=near_out.at[pl.ds(low, count)],
            dst_ref=near_in.at[pl.ds(low, count)],
            send_sem=near_send.at[i],
            recv_sem=near_recv.at[i],
            device_id=near,
            device_id_type=MESH,
        )

    def send_far(z):
        for i, target in enumerate(FAR_SENDS[z]):
            block = gathered(*target)
            if target == (z, z):
                line = jnp.sum(jnp.where(on_diagonal, block, 0.0), axis=0, keepdims=True)
                far_line_out[z] = jnp.broadcast_to(line, (8, B))
                block = jnp.where(on_diagonal, 0.0, block)
            far_out[STARTS[z] + i] = block.astype(BF16)
        for copy in far_contributions(z):
            copy.start()

    def send_near(i):
        for n, target in enumerate(NEAR_SENDS[i]):
            near_out[i * len(NEAR_SENDS[0]) + n] = gathered(*target)
        near_contribution(i).start()

    def far_halo(group):
        low = W - 1 - group
        for arrival in far_arrivals[group]:
            arrival.wait_recv()
        for o in range(W + 1):
            symmetrize(low, o)

    last = ROWS - 1
    assemble(last)
    iterate(last, range(ITERS))
    send_near(0)
    far_halo(0)
    assemble(2)
    iterate(2, range(EARLY))
    far_halo(1)
    far_halo(2)
    assemble(0)
    assemble(1)
    iterate(0, range(ITERS))
    send_far(0)
    iterate(1, range(ITERS))
    send_far(1)
    iterate(2, range(EARLY, ITERS))
    send_far(2)
    send_near(1)

    def spot(row, col):
        return mirrored(row - W, ROWS - 1), mirrored(col - row + W, BAND - 1)

    for row in range(W, W + ROWS):
        for col in range(row - W, row + W + 1):
            r, s = spot(row, col)
            owned[r, s] = gathered(row, col)

    def add_far(z):
        for copy in far_contributions(z):
            copy.wait_recv()
        for i, (row, col) in enumerate(FAR_SENDS[z]):
            block = far_in[STARTS[z] + i].astype(F32)
            if row == col:
                block = jnp.where(on_diagonal, far_line_in[z, 0:1, :], block)
            r, s = spot(5 - row, 5 - col)
            owned[r, s] += block

    def add_near(i):
        near_contribution(i).wait_recv()
        for n, (row, col) in enumerate(NEAR_SENDS[i]):
            r, s = spot(13 - row, 13 - col)
            owned[r, s] += near_in[i * len(NEAR_SENDS[0]) + n]

    add_near(0)
    add_far(0)
    add_far(1)
    add_near(1)
    add_far(2)
    for copy in near_copies + sum(far_copies, []):
        copy.wait_send()
    for z in range(W):
        for copy in far_contributions(z):
            copy.wait_send()
    for i in range(2):
        near_contribution(i).wait_send()


def on_device(hamiltonian, lists, scales, weights):
    hbm = pl.BlockSpec(memory_space=pl.ANY)
    operands = [
        pltpu.with_memory_space_constraint(value, pltpu.HBM)
        for value in (lists, weights, scales, hamiltonian)
    ]
    size = LIST * B
    return pl.pallas_call(
        kernel,
        name="density",
        out_shape=jax.ShapeDtypeStruct((ROWS, BAND, B, B), F32),
        in_specs=[hbm] * 4,
        out_specs=pl.BlockSpec(memory_space=pltpu.VMEM),
        scratch_shapes=[
            pltpu.SMEM((ROWS, LIST), jnp.int32),
            pltpu.SMEM((ROWS, LIST), F32),
            pltpu.SMEM((ROWS,), F32),
            pltpu.VMEM((EXT, BAND, B, B), BF16),
            pltpu.VMEM((EXT, BAND, B, B), F32),
            pltpu.VMEM((ROWS, size, size), F32),
            pltpu.VMEM((ROWS, 2, size, size), BF16),
            pltpu.VMEM((ROWS, 2, size, size), BF16),
            pltpu.VMEM((ROWS * LIST * LIST, B, B), F32),
            pltpu.VMEM((len(FAR), B, B), BF16),
            pltpu.VMEM((W, 8, B), F32),
            pltpu.VMEM((len(NEAR), B, B), F32),
            pltpu.VMEM((len(FAR), B, B), BF16),
            pltpu.VMEM((W, 8, B), F32),
            pltpu.VMEM((len(NEAR), B, B), F32),
            pltpu.SemaphoreType.DMA((3,)),
            pltpu.SemaphoreType.DMA,
            pltpu.SemaphoreType.DMA((9,)),
            pltpu.SemaphoreType.DMA((9,)),
            pltpu.SemaphoreType.DMA((W, 2)),
            pltpu.SemaphoreType.DMA((W, 2)),
            pltpu.SemaphoreType.DMA((2,)),
            pltpu.SemaphoreType.DMA((2,)),
        ],
        compiler_params=pltpu.CompilerParams(
            collective_id=0, has_side_effects=True, vmem_limit_bytes=40 << 20
        ),
    )(*operands)


def solution(mesh):
    in_specs = (
        P(("blk", "rep"), None, None, None),
        P(("blk", "rep"), None),
        P(("blk", "rep")),
        P(("blk", "rep"), None),
    )
    out_specs = P(("blk", "rep"), None, None, None)
    return jax.shard_map(
        on_device, mesh=mesh, in_specs=in_specs, out_specs=out_specs, check_vma=False
    )
```

```python
import jax
import jax.numpy as jnp
from jax import lax
from jax.experimental import pallas as pl
from jax.experimental.pallas import tpu as pltpu
from jax.sharding import PartitionSpec as P

B = 128
LIST = 4
W = 3
ITERS = 5
BAND = 7
ROWS = 4
EXT = ROWS + 2 * W
F32 = jnp.float32
BF16 = jnp.bfloat16
MESH = pl.DeviceIdType.MESH


def terms(row, col):
    low, high = min(row, col), max(row, col)
    return [z for z in range(ROWS) if z <= low and high <= z + 2 * W]


FAR = [(r, c) for r in range(W) for c in range(r + W + 1)]
NEAR = [(9 - r, 9 - c) for r, c in FAR]
FAR_SENDS = [[t for t in FAR if max(terms(*t)) == z] for z in range(W)]
NEAR_SENDS = [
    [t for t in NEAR if terms(*t) == [ROWS - 1]],
    [t for t in NEAR if terms(*t) != [ROWS - 1]],
]
STARTS = [0, 6, 11]
MIRRORED = [(a, b) for a in range(LIST // 2, LIST) for b in range(LIST // 2)]
EARLY = 3


def kernel(
    lists_hbm, weights_hbm, scales_hbm, ham, owned, lists, weights, scales, window, sym, xs, ys, qs, result,
    far_out, far_line_out, near_out, far_in, far_line_in, near_in,
    ready, small_sem, load_sem, halo_send, halo_recv, far_send, far_recv, near_send, near_recv,
):
    chip = lax.axis_index("blk")
    core = lax.axis_index("rep")
    chips = lax.axis_size("blk")
    total = ROWS * 2 * chips
    first = (chip * 2 + core) * ROWS
    near = (chip, 1 - core)
    far = (lax.rem(chip + 2 * core - 1 + chips, chips), 1 - core)

    def mirrored(value, last):
        return value + core * (last - 2 * value)

    barrier = pltpu.get_barrier_semaphore()
    for device in (far, near):
        pl.semaphore_signal(barrier, inc=1, device_id=device, device_id_type=MESH)
    small = [
        pltpu.make_async_copy(source, target, small_sem.at[i])
        for i, (source, target) in enumerate(
            ((lists_hbm, lists), (weights_hbm, weights), (scales_hbm, scales))
        )
    ]
    for copy in small:
        copy.start()
    load = pltpu.make_async_copy(ham, window.at[pl.ds(W, ROWS)], load_sem)
    load.start()
    for copy in small:
        copy.wait()

    position, place, share, member = [], [], [], []
    for z in range(ROWS):
        j = mirrored(z, ROWS - 1)
        spots = []
        for a in range(LIST):
            e = jnp.clip(lax.rem(lists[j, a] - first + W + total, total), 0, EXT - 1)
            spots.append(mirrored(e, EXT - 1))
        position.append(spots)
        places, shares, members = [], [], []
        for u in range(2 * W + 1):
            where = jnp.int32(0)
            weight = jnp.float32(0.0)
            here = jnp.float32(0.0)
            for a in range(LIST):
                hit = spots[a] == z + u
                where = jnp.where(hit, jnp.int32(a), where)
                weight = jnp.where(hit, weights[j, a], weight)
                here = jnp.where(hit, jnp.float32(1.0), here)
            places.append(where)
            shares.append(weight)
            members.append(here)
        place.append(places)
        share.append(shares)
        member.append(members)

    @pl.when(core == 1)
    def _():
        pl.semaphore_wait(barrier, 2)
        pl.semaphore_signal(ready, inc=1, device_id=near, device_id_type=MESH)

    @pl.when(core == 0)
    def _():
        pl.semaphore_wait(ready, 1)

    far_runs = [[(2, 3, 4)], [(1, 3, 4), (2, 2, 1)], [(0, 3, 4), (1, 2, 1), (2, 1, 1)]]
    near_runs = [[(7, 0, 6), (8, 0, 5), (9, 0, 4)]]

    def halo(runs, device, corner, index):
        copies, arrivals = [], []
        for y, slot, count in runs:
            flipped = BAND - slot - count
            low = core * slot + (1 - core) * flipped
            low_here = (1 - core) * slot + core * flipped
            row = mirrored(corner - y, EXT - 1) - W
            there = core * y + (1 - core) * (EXT - 1 - y)
            for dst, source, kept in ((there, low, copies), (mirrored(y, EXT - 1), low_here, arrivals)):
                kept.append(pltpu.make_async_remote_copy(
                    src_ref=ham.at[row, pl.ds(source, count)],
                    dst_ref=window.at[dst, pl.ds(source, count)],
                    send_sem=halo_send.at[index],
                    recv_sem=halo_recv.at[index],
                    device_id=device,
                    device_id_type=MESH,
                ))
            index += 1
        return copies, arrivals

    near_copies, near_arrivals = halo(near_runs[0], near, 13, 0)
    far_copies, far_arrivals = [], []
    index = 3
    for runs in far_runs:
        copies, arrivals = halo(runs, far, 5, index)
        far_copies.append(copies)
        far_arrivals.append(arrivals)
        index += len(runs)
    for copy in near_copies:
        copy.start()

    @pl.when(core == 0)
    def _():
        pl.semaphore_wait(barrier, 2)

    for copy in sum(far_copies, []):
        copy.start()

    def symmetrize(low, o):
        high = low + o
        slot = W + o * (1 - 2 * core)
        upper = window[mirrored(low, EXT - 1), slot]
        lower = window[mirrored(high, EXT - 1), 2 * W - slot]
        both = 0.5 * (upper.astype(F32) + lower.T.astype(F32))
        sym[low, W + o] = both
        if o:
            sym[high, W - o] = 0.5 * (lower.astype(F32) + upper.T.astype(F32))

    load.wait()
    for o in range(W + 1):
        for low in range(W, W + ROWS - o):
            symmetrize(low, o)
    for arrival in near_arrivals:
        arrival.wait_recv()
    for o in range(W + 1):
        for high in range(W + ROWS, EXT):
            symmetrize(high - o, o)

    on_diagonal = (
        lax.broadcasted_iota(jnp.int32, (B, B), 0) == lax.broadcasted_iota(jnp.int32, (B, B), 1)
    )
    diagonal = on_diagonal.astype(F32)
    size, half = LIST * B, LIST * B // 2

    def assemble(z):
        spots = position[z]
        scale = scales[mirrored(z, ROWS - 1)]
        for a in range(LIST):
            for b in range(LIST):
                offset = spots[b] - spots[a]
                stored = jnp.where(jnp.abs(offset) <= W, scale, jnp.float32(0.0))
                slot = jnp.clip(offset + W, 0, BAND - 1)
                block = stored * sym[spots[a], slot]
                if (a, b) not in MIRRORED:
                    xs[z, a * B : a * B + B, b * B : b * B + B] = block
                ys[z, 0, a * B : a * B + B, b * B : b * B + B] = block.astype(BF16)

    low, high, whole = slice(0, half), slice(half, size), slice(0, size)
    quarters = ((low, high), (high, high), (low, low))

    def iterate(z, steps):
        base = z * LIST * LIST
        for k in steps:
            now, later = k % 2, (k + 1) % 2
            for rows, cols in quarters:
                square = jnp.dot(
                    ys[z, now, rows, whole], ys[z, now, whole, cols], preferred_element_type=F32
                ).astype(BF16)
                qs[z, now, rows, cols] = square
                if rows != cols:
                    qs[z, now, cols, rows] = square.T
            for rows, cols in quarters:
                value = 1.5 * xs[z, rows, cols] - 0.5 * jnp.dot(
                    ys[z, now, rows, whole], qs[z, now, whole, cols], preferred_element_type=F32
                )
                if k < ITERS - 1:
                    xs[z, rows, cols] = value
                    rounded = value.astype(BF16)
                    ys[z, later, rows, cols] = rounded
                    if rows != cols:
                        ys[z, later, cols, rows] = rounded.T
                    continue
                for m in range(LIST // 2):
                    for n in range(LIST // 2):
                        a, b = rows.start // B + m, cols.start // B + n
                        block = value[m * B : m * B + B, n * B : n * B + B]
                        block = 0.5 * (diagonal - block) if a == b else -0.5 * block
                        result[base + a * LIST + b] = block
                        if rows != cols:
                            result[base + b * LIST + a] = block.T

    def gathered(row, col):
        value = None
        for z in terms(row, col):
            u, v = row - z, col - z
            factor = share[z][u] * member[z][v]
            term = factor * result[z * LIST * LIST + place[z][u] * LIST + place[z][v]]
            value = term if value is None else value + term
        return value

    def far_contributions(z):
        low, count = STARTS[z], len(FAR_SENDS[z])
        return [
            pltpu.make_async_remote_copy(
                src_ref=source,
                dst_ref=target,
                send_sem=far_send.at[z, i],
                recv_sem=far_recv.at[z, i],
                device_id=far,
                device_id_type=MESH,
            )
            for i, (source, target) in enumerate((
                (far_line_out.at[z], far_line_in.at[z]),
                (far_out.at[pl.ds(low, count)], far_in.at[pl.ds(low, count)]),
            ))
        ]

    def near_contribution(i):
        low, count = i * len(NEAR_SENDS[0]), len(NEAR_SENDS[i])
        return pltpu.make_async_remote_copy(
            src_ref=near_out.at[pl.ds(low, count)],
            dst_ref=near_in.at[pl.ds(low, count)],
            send_sem=near_send.at[i],
            recv_sem=near_recv.at[i],
            device_id=near,
            device_id_type=MESH,
        )

    def send_far(z):
        for i, target in enumerate(FAR_SENDS[z]):
            block = gathered(*target)
            if target == (z, z):
                line = jnp.sum(jnp.where(on_diagonal, block, 0.0), axis=0, keepdims=True)
                far_line_out[z] = jnp.broadcast_to(line, (8, B))
                block = jnp.where(on_diagonal, 0.0, block)
            far_out[STARTS[z] + i] = block.astype(BF16)
        for copy in far_contributions(z):
            copy.start()

    def send_near(i):
        for n, target in enumerate(NEAR_SENDS[i]):
            near_out[i * len(NEAR_SENDS[0]) + n] = gathered(*target)
        near_contribution(i).start()

    def far_halo(group):
        low = W - 1 - group
        for arrival in far_arrivals[group]:
            arrival.wait_recv()
        for o in range(W + 1):
            symmetrize(low, o)

    last = ROWS - 1
    assemble(last)
    iterate(last, range(ITERS))
    send_near(0)
    far_halo(0)
    assemble(2)
    iterate(2, range(EARLY))
    far_halo(1)
    assemble(1)
    iterate(1, range(2))
    far_halo(2)
    assemble(0)
    iterate(0, range(ITERS))
    send_far(0)
    iterate(1, range(2, ITERS))
    send_far(1)
    iterate(2, range(EARLY, ITERS))
    send_far(2)
    send_near(1)

    def spot(row, col):
        return mirrored(row - W, ROWS - 1), mirrored(col - row + W, BAND - 1)

    for row in range(W, W + ROWS):
        for col in range(row - W, row + W + 1):
            r, s = spot(row, col)
            owned[r, s] = gathered(row, col)

    def add_far(z):
        for copy in far_contributions(z):
            copy.wait_recv()
        for i, (row, col) in enumerate(FAR_SENDS[z]):
            block = far_in[STARTS[z] + i].astype(F32)
            if row == col:
                block = jnp.where(on_diagonal, far_line_in[z, 0:1, :], block)
            r, s = spot(5 - row, 5 - col)
            owned[r, s] += block

    def add_near(i):
        near_contribution(i).wait_recv()
        for n, (row, col) in enumerate(NEAR_SENDS[i]):
            r, s = spot(13 - row, 13 - col)
            owned[r, s] += near_in[i * len(NEAR_SENDS[0]) + n]

    add_near(0)
    add_far(0)
    add_far(1)
    add_near(1)
    add_far(2)
    for copy in near_copies + sum(far_copies, []):
        copy.wait_send()
    for z in range(W):
        for copy in far_contributions(z):
            copy.wait_send()
    for i in range(2):
        near_contribution(i).wait_send()


def on_device(hamiltonian, lists, scales, weights):
    hbm = pl.BlockSpec(memory_space=pl.ANY)
    operands = [
        pltpu.with_memory_space_constraint(value, pltpu.HBM)
        for value in (lists, weights, scales, hamiltonian)
    ]
    size = LIST * B
    return pl.pallas_call(
        kernel,
        name="density",
        out_shape=jax.ShapeDtypeStruct((ROWS, BAND, B, B), F32),
        in_specs=[hbm] * 4,
        out_specs=pl.BlockSpec(memory_space=pltpu.VMEM),
        scratch_shapes=[
            pltpu.SMEM((ROWS, LIST), jnp.int32),
            pltpu.SMEM((ROWS, LIST), F32),
            pltpu.SMEM((ROWS,), F32),
            pltpu.VMEM((EXT, BAND, B, B), BF16),
            pltpu.VMEM((EXT, BAND, B, B), F32),
            pltpu.VMEM((ROWS, size, size), F32),
            pltpu.VMEM((ROWS, 2, size, size), BF16),
            pltpu.VMEM((ROWS, 2, size, size), BF16),
            pltpu.VMEM((ROWS * LIST * LIST, B, B), F32),
            pltpu.VMEM((len(FAR), B, B), BF16),
            pltpu.VMEM((W, 8, B), F32),
            pltpu.VMEM((len(NEAR), B, B), F32),
            pltpu.VMEM((len(FAR), B, B), BF16),
            pltpu.VMEM((W, 8, B), F32),
            pltpu.VMEM((len(NEAR), B, B), F32),
            pltpu.SemaphoreType.REGULAR,
            pltpu.SemaphoreType.DMA((3,)),
            pltpu.SemaphoreType.DMA,
            pltpu.SemaphoreType.DMA((9,)),
            pltpu.SemaphoreType.DMA((9,)),
            pltpu.SemaphoreType.DMA((W, 2)),
            pltpu.SemaphoreType.DMA((W, 2)),
            pltpu.SemaphoreType.DMA((2,)),
            pltpu.SemaphoreType.DMA((2,)),
        ],
        compiler_params=pltpu.CompilerParams(
            collective_id=0, has_side_effects=True, vmem_limit_bytes=40 << 20
        ),
    )(*operands)


def solution(mesh):
    in_specs = (
        P(("blk", "rep"), None, None, None),
        P(("blk", "rep"), None),
        P(("blk", "rep")),
        P(("blk", "rep"), None),
    )
    out_specs = P(("blk", "rep"), None, None, None)
    return jax.shard_map(
        on_device, mesh=mesh, in_specs=in_specs, out_specs=out_specs, check_vma=False
    )
```

```python
import jax
import jax.numpy as jnp
from jax import lax
from jax.experimental import pallas as pl
from jax.experimental.pallas import tpu as pltpu
from jax.sharding import PartitionSpec as P

B = 128
LIST = 4
W = 3
ITERS = 5
BAND = 7
ROWS = 4
EXT = ROWS + 2 * W
F32 = jnp.float32
BF16 = jnp.bfloat16
MESH = pl.DeviceIdType.MESH


def terms(row, col):
    low, high = min(row, col), max(row, col)
    return [z for z in range(ROWS) if z <= low and high <= z + 2 * W]


FAR = [(r, c) for r in range(W) for c in range(r + W + 1)]
NEAR = [(9 - r, 9 - c) for r, c in FAR]
FAR_SENDS = [[t for t in FAR if max(terms(*t)) == z] for z in range(W)]
NEAR_SENDS = [
    [t for t in NEAR if terms(*t) == [ROWS - 1]],
    [t for t in NEAR if terms(*t) != [ROWS - 1]],
]
FAR_SENDS[0] = [(0, 0), (0, 3), (0, 1), (0, 2)]
SHARED = [(0, 1), (0, 2)]
STARTS = [0, 4, 9]
FAR_BLOCKS = 13
MIRRORED = [(a, b) for a in range(LIST // 2, LIST) for b in range(LIST // 2)]
EARLY = 3


def kernel(
    lists_hbm, weights_hbm, scales_hbm, ham, owned, lists, weights, scales, window, sym, xs, ys, qs, result,
    far_out, far_line_out, near_out, far_in, far_line_in, near_in,
    ready, small_sem, load_sem, halo_send, halo_recv, far_send, far_recv, near_send, near_recv,
):
    chip = lax.axis_index("blk")
    core = lax.axis_index("rep")
    chips = lax.axis_size("blk")
    total = ROWS * 2 * chips
    first = (chip * 2 + core) * ROWS
    near = (chip, 1 - core)
    far = (lax.rem(chip + 2 * core - 1 + chips, chips), 1 - core)

    def mirrored(value, last):
        return value + core * (last - 2 * value)

    barrier = pltpu.get_barrier_semaphore()
    for device in (far, near):
        pl.semaphore_signal(barrier, inc=1, device_id=device, device_id_type=MESH)
    small = [
        pltpu.make_async_copy(source, target, small_sem.at[i])
        for i, (source, target) in enumerate(
            ((lists_hbm, lists), (weights_hbm, weights), (scales_hbm, scales))
        )
    ]
    for copy in small:
        copy.start()
    load = pltpu.make_async_copy(ham, window.at[pl.ds(W, ROWS)], load_sem)
    load.start()
    for copy in small:
        copy.wait()

    position, place, share, member = [], [], [], []
    for z in range(ROWS):
        j = mirrored(z, ROWS - 1)
        spots = []
        for a in range(LIST):
            e = jnp.clip(lax.rem(lists[j, a] - first + W + total, total), 0, EXT - 1)
            spots.append(mirrored(e, EXT - 1))
        position.append(spots)
        places, shares, members = [], [], []
        for u in range(2 * W + 1):
            where = jnp.int32(0)
            weight = jnp.float32(0.0)
            here = jnp.float32(0.0)
            for a in range(LIST):
                hit = spots[a] == z + u
                where = jnp.where(hit, jnp.int32(a), where)
                weight = jnp.where(hit, weights[j, a], weight)
                here = jnp.where(hit, jnp.float32(1.0), here)
            places.append(where)
            shares.append(weight)
            members.append(here)
        place.append(places)
        share.append(shares)
        member.append(members)

    @pl.when(core == 1)
    def _():
        pl.semaphore_wait(barrier, 2)
        pl.semaphore_signal(ready, inc=1, device_id=near, device_id_type=MESH)

    @pl.when(core == 0)
    def _():
        pl.semaphore_wait(ready, 1)

    far_runs = [[(2, 3, 4)], [(1, 3, 4), (2, 2, 1)], [(0, 3, 4), (1, 2, 1), (2, 1, 1)]]
    near_runs = [[(7, 0, 6), (8, 0, 5), (9, 0, 4)]]

    def halo(runs, device, corner, index):
        copies, arrivals = [], []
        for y, slot, count in runs:
            flipped = BAND - slot - count
            low = core * slot + (1 - core) * flipped
            low_here = (1 - core) * slot + core * flipped
            row = mirrored(corner - y, EXT - 1) - W
            there = core * y + (1 - core) * (EXT - 1 - y)
            for dst, source, kept in ((there, low, copies), (mirrored(y, EXT - 1), low_here, arrivals)):
                kept.append(pltpu.make_async_remote_copy(
                    src_ref=ham.at[row, pl.ds(source, count)],
                    dst_ref=window.at[dst, pl.ds(source, count)],
                    send_sem=halo_send.at[index],
                    recv_sem=halo_recv.at[index],
                    device_id=device,
                    device_id_type=MESH,
                ))
            index += 1
        return copies, arrivals

    near_copies, near_arrivals = halo(near_runs[0], near, 13, 0)
    far_copies, far_arrivals = [], []
    index = 3
    for runs in far_runs:
        copies, arrivals = halo(runs, far, 5, index)
        far_copies.append(copies)
        far_arrivals.append(arrivals)
        index += len(runs)
    for copy in near_copies:
        copy.start()

    @pl.when(core == 0)
    def _():
        pl.semaphore_wait(barrier, 2)

    for copy in sum(far_copies, []):
        copy.start()

    def symmetrize(low, o):
        high = low + o
        slot = W + o * (1 - 2 * core)
        upper = window[mirrored(low, EXT - 1), slot]
        lower = window[mirrored(high, EXT - 1), 2 * W - slot]
        both = 0.5 * (upper.astype(F32) + lower.T.astype(F32))
        sym[low, W + o] = both
        if o:
            sym[high, W - o] = 0.5 * (lower.astype(F32) + upper.T.astype(F32))

    load.wait()
    for o in range(W + 1):
        for low in range(W, W + ROWS - o):
            symmetrize(low, o)
    for arrival in near_arrivals:
        arrival.wait_recv()
    for o in range(W + 1):
        for high in range(W + ROWS, EXT):
            symmetrize(high - o, o)

    on_diagonal = (
        lax.broadcasted_iota(jnp.int32, (B, B), 0) == lax.broadcasted_iota(jnp.int32, (B, B), 1)
    )
    diagonal = on_diagonal.astype(F32)
    size, half = LIST * B, LIST * B // 2

    def assemble(z):
        spots = position[z]
        scale = scales[mirrored(z, ROWS - 1)]
        for a in range(LIST):
            for b in range(LIST):
                offset = spots[b] - spots[a]
                stored = jnp.where(jnp.abs(offset) <= W, scale, jnp.float32(0.0))
                slot = jnp.clip(offset + W, 0, BAND - 1)
                block = stored * sym[spots[a], slot]
                if (a, b) not in MIRRORED:
                    xs[z, a * B : a * B + B, b * B : b * B + B] = block
                ys[z, 0, a * B : a * B + B, b * B : b * B + B] = block.astype(BF16)

    low, high, whole = slice(0, half), slice(half, size), slice(0, size)
    quarters = ((low, high), (high, high), (low, low))

    def iterate(z, steps):
        base = z * LIST * LIST
        for k in steps:
            now, later = k % 2, (k + 1) % 2
            for rows, cols in quarters:
                square = jnp.dot(
                    ys[z, now, rows, whole], ys[z, now, whole, cols], preferred_element_type=F32
                ).astype(BF16)
                qs[z, now, rows, cols] = square
                if rows != cols:
                    qs[z, now, cols, rows] = square.T
            for rows, cols in quarters:
                value = 1.5 * xs[z, rows, cols] - 0.5 * jnp.dot(
                    ys[z, now, rows, whole], qs[z, now, whole, cols], preferred_element_type=F32
                )
                if k < ITERS - 1:
                    xs[z, rows, cols] = value
                    rounded = value.astype(BF16)
                    ys[z, later, rows, cols] = rounded
                    if rows != cols:
                        ys[z, later, cols, rows] = rounded.T
                    continue
                for m in range(LIST // 2):
                    for n in range(LIST // 2):
                        a, b = rows.start // B + m, cols.start // B + n
                        block = value[m * B : m * B + B, n * B : n * B + B]
                        block = 0.5 * (diagonal - block) if a == b else -0.5 * block
                        result[base + a * LIST + b] = block
                        if rows != cols:
                            result[base + b * LIST + a] = block.T

    def gathered(row, col):
        value = None
        for z in terms(row, col):
            u, v = row - z, col - z
            factor = share[z][u] * member[z][v]
            term = factor * result[z * LIST * LIST + place[z][u] * LIST + place[z][v]]
            value = term if value is None else value + term
        return value

    def far_contributions(z):
        ends = [0, 2, 4] if z == 0 else [0, len(FAR_SENDS[z])]
        runs = [pl.ds(STARTS[z] + low, high - low) for low, high in zip(ends, ends[1:])]
        return [
            pltpu.make_async_remote_copy(
                src_ref=source,
                dst_ref=target,
                send_sem=far_send.at[z, i],
                recv_sem=far_recv.at[z, i],
                device_id=far,
                device_id_type=MESH,
            )
            for i, (source, target) in enumerate(
                [(far_line_out.at[z], far_line_in.at[z])]
                + [(far_out.at[run], far_in.at[run]) for run in runs]
            )
        ]

    def near_contribution(i):
        low, count = i * len(NEAR_SENDS[0]), len(NEAR_SENDS[i])
        return pltpu.make_async_remote_copy(
            src_ref=near_out.at[pl.ds(low, count)],
            dst_ref=near_in.at[pl.ds(low, count)],
            send_sem=near_send.at[i],
            recv_sem=near_recv.at[i],
            device_id=near,
            device_id_type=MESH,
        )

    def send_far(z):
        copies = far_contributions(z)
        for i, target in enumerate(FAR_SENDS[z]):
            if target in SHARED:
                u, v = target
                factor = member[z][u] * member[z][v]
                block = factor * result[z * LIST * LIST + place[z][u] * LIST + place[z][v]]
            else:
                block = gathered(*target)
            if target == (z, z):
                line = jnp.sum(jnp.where(on_diagonal, block, 0.0), axis=0, keepdims=True)
                lines = jnp.broadcast_to(line, (8, B))
                if z == 0:
                    row = lax.broadcasted_iota(jnp.int32, (8, B), 0)
                    for u in range(W):
                        lines = jnp.where(row == u + 1, share[z][u], lines)
                far_line_out[z] = lines
                block = jnp.where(on_diagonal, 0.0, block)
            far_out[STARTS[z] + i] = block.astype(BF16)
            if z == 0 and i == 1:
                copies[1].start()
        copies[-1].start()
        copies[0].start()

    def send_near(i):
        for n, target in enumerate(NEAR_SENDS[i]):
            near_out[i * len(NEAR_SENDS[0]) + n] = gathered(*target)
        near_contribution(i).start()

    def far_halo(group):
        low = W - 1 - group
        for arrival in far_arrivals[group]:
            arrival.wait_recv()
        for o in range(W + 1):
            symmetrize(low, o)

    last = ROWS - 1
    assemble(last)
    iterate(last, range(ITERS))
    send_near(0)
    far_halo(0)
    assemble(2)
    iterate(2, range(EARLY))
    far_halo(1)
    assemble(1)
    iterate(1, range(3))
    far_halo(2)
    assemble(0)
    iterate(0, range(ITERS))
    send_far(0)
    iterate(1, range(3, ITERS))
    send_far(1)
    iterate(2, range(EARLY, ITERS))
    send_far(2)
    send_near(1)

    def spot(row, col):
        return mirrored(row - W, ROWS - 1), mirrored(col - row + W, BAND - 1)

    for row in range(W, W + ROWS):
        for col in range(row - W, row + W + 1):
            r, s = spot(row, col)
            owned[r, s] = gathered(row, col)

    def add_far(z):
        for copy in far_contributions(z):
            copy.wait_recv()
        for i, (row, col) in enumerate(FAR_SENDS[z]):
            block = far_in[STARTS[z] + i].astype(F32)
            if (row, col) in SHARED:
                r, s = spot(5 - col, 5 - row)
                owned[r, s] += far_line_in[z, 1 + col : 2 + col, :] * block.T
                block = far_line_in[z, 1 + row : 2 + row, :] * block
            if row == col:
                block = jnp.where(on_diagonal, far_line_in[z, 0:1, :], block)
            r, s = spot(5 - row, 5 - col)
            owned[r, s] += block

    def add_near(i):
        near_contribution(i).wait_recv()
        for n, (row, col) in enumerate(NEAR_SENDS[i]):
            r, s = spot(13 - row, 13 - col)
            owned[r, s] += near_in[i * len(NEAR_SENDS[0]) + n]

    add_near(0)
    add_far(0)
    add_far(1)
    add_near(1)
    add_far(2)
    for copy in near_copies + sum(far_copies, []):
        copy.wait_send()
    for z in range(W):
        for copy in far_contributions(z):
            copy.wait_send()
    for i in range(2):
        near_contribution(i).wait_send()


def on_device(hamiltonian, lists, scales, weights):
    hbm = pl.BlockSpec(memory_space=pl.ANY)
    operands = [
        pltpu.with_memory_space_constraint(value, pltpu.HBM)
        for value in (lists, weights, scales, hamiltonian)
    ]
    size = LIST * B
    return pl.pallas_call(
        kernel,
        name="density",
        out_shape=jax.ShapeDtypeStruct((ROWS, BAND, B, B), F32),
        in_specs=[hbm] * 4,
        out_specs=pl.BlockSpec(memory_space=pltpu.VMEM),
        scratch_shapes=[
            pltpu.SMEM((ROWS, LIST), jnp.int32),
            pltpu.SMEM((ROWS, LIST), F32),
            pltpu.SMEM((ROWS,), F32),
            pltpu.VMEM((EXT, BAND, B, B), BF16),
            pltpu.VMEM((EXT, BAND, B, B), F32),
            pltpu.VMEM((ROWS, size, size), F32),
            pltpu.VMEM((ROWS, 2, size, size), BF16),
            pltpu.VMEM((ROWS, 2, size, size), BF16),
            pltpu.VMEM((ROWS * LIST * LIST, B, B), F32),
            pltpu.VMEM((FAR_BLOCKS, B, B), BF16),
            pltpu.VMEM((W, 8, B), F32),
            pltpu.VMEM((len(NEAR), B, B), F32),
            pltpu.VMEM((FAR_BLOCKS, B, B), BF16),
            pltpu.VMEM((W, 8, B), F32),
            pltpu.VMEM((len(NEAR), B, B), F32),
            pltpu.SemaphoreType.REGULAR,
            pltpu.SemaphoreType.DMA((3,)),
            pltpu.SemaphoreType.DMA,
            pltpu.SemaphoreType.DMA((9,)),
            pltpu.SemaphoreType.DMA((9,)),
            pltpu.SemaphoreType.DMA((W, W)),
            pltpu.SemaphoreType.DMA((W, W)),
            pltpu.SemaphoreType.DMA((2,)),
            pltpu.SemaphoreType.DMA((2,)),
        ],
        compiler_params=pltpu.CompilerParams(
            collective_id=0, has_side_effects=True, vmem_limit_bytes=40 << 20
        ),
    )(*operands)


def solution(mesh):
    in_specs = (
        P(("blk", "rep"), None, None, None),
        P(("blk", "rep"), None),
        P(("blk", "rep")),
        P(("blk", "rep"), None),
    )
    out_specs = P(("blk", "rep"), None, None, None)
    return jax.shard_map(
        on_device, mesh=mesh, in_specs=in_specs, out_specs=out_specs, check_vma=False
    )
```

```python
import jax
import jax.numpy as jnp
from jax import lax
from jax.experimental import pallas as pl
from jax.experimental.pallas import tpu as pltpu
from jax.sharding import PartitionSpec as P

B = 128
LIST = 4
W = 3
ITERS = 5
BAND = 7
ROWS = 4
EXT = ROWS + 2 * W
F32 = jnp.float32
BF16 = jnp.bfloat16
MESH = pl.DeviceIdType.MESH


def terms(row, col):
    low, high = min(row, col), max(row, col)
    return [z for z in range(ROWS) if z <= low and high <= z + 2 * W]


FAR = [(r, c) for r in range(W) for c in range(r + W + 1)]
NEAR = [(9 - r, 9 - c) for r, c in FAR]
FAR_SENDS = [[t for t in FAR if max(terms(*t)) == z] for z in range(W)]
NEAR_SENDS = [
    [t for t in NEAR if terms(*t) == [ROWS - 1]],
    [t for t in NEAR if terms(*t) != [ROWS - 1]],
]
FAR_SENDS[0] = [(0, 0), (0, 3), (0, 1), (0, 2)]
SHARED = [(0, 1), (0, 2)]
STARTS = [0, 4, 9]
FAR_BLOCKS = 13
MIRRORED = [(a, b) for a in range(LIST // 2, LIST) for b in range(LIST // 2)]
EARLY = 4


def kernel(
    lists_hbm, weights_hbm, scales_hbm, ham, owned, lists, weights, scales, window, sym, xs, ys, qs, result,
    far_out, far_line_out, near_out, far_in, far_line_in, near_in,
    ready, small_sem, load_sem, halo_send, halo_recv, far_send, far_recv, near_send, near_recv,
):
    chip = lax.axis_index("blk")
    core = lax.axis_index("rep")
    chips = lax.axis_size("blk")
    total = ROWS * 2 * chips
    first = (chip * 2 + core) * ROWS
    near = (chip, 1 - core)
    far = (lax.rem(chip + 2 * core - 1 + chips, chips), 1 - core)

    def mirrored(value, last):
        return value + core * (last - 2 * value)

    barrier = pltpu.get_barrier_semaphore()
    for device in (far, near):
        pl.semaphore_signal(barrier, inc=1, device_id=device, device_id_type=MESH)
    small = [
        pltpu.make_async_copy(source, target, small_sem.at[i])
        for i, (source, target) in enumerate(
            ((lists_hbm, lists), (weights_hbm, weights), (scales_hbm, scales))
        )
    ]
    for copy in small:
        copy.start()
    load = pltpu.make_async_copy(ham, window.at[pl.ds(W, ROWS)], load_sem)
    load.start()
    for copy in small:
        copy.wait()

    position, place, share, member = [], [], [], []
    for z in range(ROWS):
        j = mirrored(z, ROWS - 1)
        spots = []
        for a in range(LIST):
            e = jnp.clip(lax.rem(lists[j, a] - first + W + total, total), 0, EXT - 1)
            spots.append(mirrored(e, EXT - 1))
        position.append(spots)
        places, shares, members = [], [], []
        for u in range(2 * W + 1):
            where = jnp.int32(0)
            weight = jnp.float32(0.0)
            here = jnp.float32(0.0)
            for a in range(LIST):
                hit = spots[a] == z + u
                where = jnp.where(hit, jnp.int32(a), where)
                weight = jnp.where(hit, weights[j, a], weight)
                here = jnp.where(hit, jnp.float32(1.0), here)
            places.append(where)
            shares.append(weight)
            members.append(here)
        place.append(places)
        share.append(shares)
        member.append(members)

    @pl.when(core == 1)
    def _():
        pl.semaphore_wait(barrier, 2)
        pl.semaphore_signal(ready, inc=1, device_id=near, device_id_type=MESH)

    @pl.when(core == 0)
    def _():
        pl.semaphore_wait(ready, 1)

    far_runs = [[(2, 3, 4)], [(1, 3, 4), (2, 2, 1)], [(0, 3, 4), (1, 2, 1), (2, 1, 1)]]
    near_runs = [[(7, 0, 6), (8, 0, 5), (9, 0, 4)]]

    def halo(runs, device, corner, index):
        copies, arrivals = [], []
        for y, slot, count in runs:
            flipped = BAND - slot - count
            low = core * slot + (1 - core) * flipped
            low_here = (1 - core) * slot + core * flipped
            row = mirrored(corner - y, EXT - 1) - W
            there = core * y + (1 - core) * (EXT - 1 - y)
            for dst, source, kept in ((there, low, copies), (mirrored(y, EXT - 1), low_here, arrivals)):
                kept.append(pltpu.make_async_remote_copy(
                    src_ref=ham.at[row, pl.ds(source, count)],
                    dst_ref=window.at[dst, pl.ds(source, count)],
                    send_sem=halo_send.at[index],
                    recv_sem=halo_recv.at[index],
                    device_id=device,
                    device_id_type=MESH,
                ))
            index += 1
        return copies, arrivals

    near_copies, near_arrivals = halo(near_runs[0], near, 13, 0)
    far_copies, far_arrivals = [], []
    index = 3
    for runs in far_runs:
        copies, arrivals = halo(runs, far, 5, index)
        far_copies.append(copies)
        far_arrivals.append(arrivals)
        index += len(runs)
    @pl.when(core == 1)
    def _():
        for copy in sum(far_copies, []) + near_copies:
            copy.start()

    @pl.when(core == 0)
    def _():
        for copy in near_copies:
            copy.start()
        pl.semaphore_wait(barrier, 2)
        for copy in sum(far_copies, []):
            copy.start()


    def symmetrize(low, o):
        high = low + o
        slot = W + o * (1 - 2 * core)
        upper = window[mirrored(low, EXT - 1), slot]
        lower = window[mirrored(high, EXT - 1), 2 * W - slot]
        both = 0.5 * (upper.astype(F32) + lower.T.astype(F32))
        sym[low, W + o] = both
        if o:
            sym[high, W - o] = 0.5 * (lower.astype(F32) + upper.T.astype(F32))

    load.wait()
    for o in range(W + 1):
        for low in range(W, W + ROWS - o):
            symmetrize(low, o)
    for arrival in near_arrivals:
        arrival.wait_recv()
    for o in range(W + 1):
        for high in range(W + ROWS, EXT):
            symmetrize(high - o, o)

    on_diagonal = (
        lax.broadcasted_iota(jnp.int32, (B, B), 0) == lax.broadcasted_iota(jnp.int32, (B, B), 1)
    )
    diagonal = on_diagonal.astype(F32)
    size, half = LIST * B, LIST * B // 2

    def assemble(z):
        spots = position[z]
        scale = scales[mirrored(z, ROWS - 1)]
        for a in range(LIST):
            for b in range(LIST):
                offset = spots[b] - spots[a]
                stored = jnp.where(jnp.abs(offset) <= W, scale, jnp.float32(0.0))
                slot = jnp.clip(offset + W, 0, BAND - 1)
                block = stored * sym[spots[a], slot]
                if (a, b) not in MIRRORED:
                    xs[z, a * B : a * B + B, b * B : b * B + B] = block
                ys[z, 0, a * B : a * B + B, b * B : b * B + B] = block.astype(BF16)

    low, high, whole = slice(0, half), slice(half, size), slice(0, size)
    quarters = ((low, high), (high, high), (low, low))

    def iterate(z, steps):
        base = z * LIST * LIST
        for k in steps:
            now, later = k % 2, (k + 1) % 2
            for rows, cols in (quarters[1], quarters[0], quarters[2]):
                square = jnp.dot(
                    ys[z, now, rows, whole], ys[z, now, whole, cols], preferred_element_type=F32
                ).astype(BF16)
                qs[z, now, rows, cols] = square
                if rows != cols:
                    qs[z, now, cols, rows] = square.T
            for rows, cols in quarters:
                value = 1.5 * xs[z, rows, cols] - 0.5 * jnp.dot(
                    ys[z, now, rows, whole], qs[z, now, whole, cols], preferred_element_type=F32
                )
                if k < ITERS - 1:
                    xs[z, rows, cols] = value
                    rounded = value.astype(BF16)
                    ys[z, later, rows, cols] = rounded
                    if rows != cols:
                        ys[z, later, cols, rows] = rounded.T
                    continue
                for m in range(LIST // 2):
                    for n in range(LIST // 2):
                        a, b = rows.start // B + m, cols.start // B + n
                        block = value[m * B : m * B + B, n * B : n * B + B]
                        block = 0.5 * (diagonal - block) if a == b else -0.5 * block
                        result[base + a * LIST + b] = block
                        if rows != cols:
                            result[base + b * LIST + a] = block.T

    def gathered(row, col):
        value = None
        for z in terms(row, col):
            u, v = row - z, col - z
            factor = share[z][u] * member[z][v]
            term = factor * result[z * LIST * LIST + place[z][u] * LIST + place[z][v]]
            value = term if value is None else value + term
        return value

    def far_contributions(z):
        ends = [0, 2, 4] if z == 0 else [0, len(FAR_SENDS[z])]
        runs = [pl.ds(STARTS[z] + low, high - low) for low, high in zip(ends, ends[1:])]
        return [
            pltpu.make_async_remote_copy(
                src_ref=source,
                dst_ref=target,
                send_sem=far_send.at[z, i],
                recv_sem=far_recv.at[z, i],
                device_id=far,
                device_id_type=MESH,
            )
            for i, (source, target) in enumerate(
                [(far_line_out.at[z], far_line_in.at[z])]
                + [(far_out.at[run], far_in.at[run]) for run in runs]
            )
        ]

    def near_contribution(i):
        low, count = i * len(NEAR_SENDS[0]), len(NEAR_SENDS[i])
        return pltpu.make_async_remote_copy(
            src_ref=near_out.at[pl.ds(low, count)],
            dst_ref=near_in.at[pl.ds(low, count)],
            send_sem=near_send.at[i],
            recv_sem=near_recv.at[i],
            device_id=near,
            device_id_type=MESH,
        )

    def send_far(z):
        copies = far_contributions(z)
        for i, target in enumerate(FAR_SENDS[z]):
            if target in SHARED:
                u, v = target
                factor = member[z][u] * member[z][v]
                block = factor * result[z * LIST * LIST + place[z][u] * LIST + place[z][v]]
            else:
                block = gathered(*target)
            if target == (z, z):
                line = jnp.sum(jnp.where(on_diagonal, block, 0.0), axis=0, keepdims=True)
                lines = jnp.broadcast_to(line, (8, B))
                if z == 0:
                    row = lax.broadcasted_iota(jnp.int32, (8, B), 0)
                    for u in range(W):
                        lines = jnp.where(row == u + 1, share[z][u], lines)
                far_line_out[z] = lines
                block = jnp.where(on_diagonal, 0.0, block)
            far_out[STARTS[z] + i] = block.astype(BF16)
            if z == 0 and i == 1:
                copies[1].start()
        copies[-1].start()
        copies[0].start()

    def send_near(i):
        for n, target in enumerate(NEAR_SENDS[i]):
            near_out[i * len(NEAR_SENDS[0]) + n] = gathered(*target)
        near_contribution(i).start()

    def far_halo(group):
        low = W - 1 - group
        for arrival in far_arrivals[group]:
            arrival.wait_recv()
        for o in range(W + 1):
            symmetrize(low, o)

    last = ROWS - 1
    assemble(last)
    iterate(last, range(ITERS))
    send_near(0)
    far_halo(0)
    assemble(2)
    iterate(2, range(EARLY))
    far_halo(1)
    assemble(1)
    iterate(1, range(3))
    far_halo(2)
    assemble(0)
    iterate(0, range(ITERS))
    send_far(0)
    iterate(1, range(3, ITERS))
    send_far(1)
    iterate(2, range(EARLY, ITERS))
    send_far(2)
    send_near(1)

    def spot(row, col):
        return mirrored(row - W, ROWS - 1), mirrored(col - row + W, BAND - 1)

    for row in range(W, W + ROWS):
        for col in range(row - W, row + W + 1):
            r, s = spot(row, col)
            owned[r, s] = gathered(row, col)

    def add_far(z):
        for copy in far_contributions(z):
            copy.wait_recv()
        for i, (row, col) in enumerate(FAR_SENDS[z]):
            block = far_in[STARTS[z] + i].astype(F32)
            if (row, col) in SHARED:
                r, s = spot(5 - col, 5 - row)
                owned[r, s] += far_line_in[z, 1 + col : 2 + col, :] * block.T
                block = far_line_in[z, 1 + row : 2 + row, :] * block
            if row == col:
                block = jnp.where(on_diagonal, far_line_in[z, 0:1, :], block)
            r, s = spot(5 - row, 5 - col)
            owned[r, s] += block

    def add_near(i):
        near_contribution(i).wait_recv()
        for n, (row, col) in enumerate(NEAR_SENDS[i]):
            r, s = spot(13 - row, 13 - col)
            owned[r, s] += near_in[i * len(NEAR_SENDS[0]) + n]

    add_near(0)
    add_far(0)
    add_far(1)
    add_near(1)
    add_far(2)
    for copy in near_copies + sum(far_copies, []):
        copy.wait_send()
    for z in range(W):
        for copy in far_contributions(z):
            copy.wait_send()
    for i in range(2):
        near_contribution(i).wait_send()


def on_device(hamiltonian, lists, scales, weights):
    hbm = pl.BlockSpec(memory_space=pl.ANY)
    operands = [
        pltpu.with_memory_space_constraint(value, pltpu.HBM)
        for value in (lists, weights, scales, hamiltonian)
    ]
    size = LIST * B
    return pl.pallas_call(
        kernel,
        name="density",
        out_shape=jax.ShapeDtypeStruct((ROWS, BAND, B, B), F32),
        in_specs=[hbm] * 4,
        out_specs=pl.BlockSpec(memory_space=pltpu.VMEM),
        scratch_shapes=[
            pltpu.SMEM((ROWS, LIST), jnp.int32),
            pltpu.SMEM((ROWS, LIST), F32),
            pltpu.SMEM((ROWS,), F32),
            pltpu.VMEM((EXT, BAND, B, B), BF16),
            pltpu.VMEM((EXT, BAND, B, B), F32),
            pltpu.VMEM((ROWS, size, size), F32),
            pltpu.VMEM((ROWS, 2, size, size), BF16),
            pltpu.VMEM((ROWS, 2, size, size), BF16),
            pltpu.VMEM((ROWS * LIST * LIST, B, B), F32),
            pltpu.VMEM((FAR_BLOCKS, B, B), BF16),
            pltpu.VMEM((W, 8, B), F32),
            pltpu.VMEM((len(NEAR), B, B), F32),
            pltpu.VMEM((FAR_BLOCKS, B, B), BF16),
            pltpu.VMEM((W, 8, B), F32),
            pltpu.VMEM((len(NEAR), B, B), F32),
            pltpu.SemaphoreType.REGULAR,
            pltpu.SemaphoreType.DMA((3,)),
            pltpu.SemaphoreType.DMA,
            pltpu.SemaphoreType.DMA((9,)),
            pltpu.SemaphoreType.DMA((9,)),
            pltpu.SemaphoreType.DMA((W, W)),
            pltpu.SemaphoreType.DMA((W, W)),
            pltpu.SemaphoreType.DMA((2,)),
            pltpu.SemaphoreType.DMA((2,)),
        ],
        compiler_params=pltpu.CompilerParams(
            collective_id=0, has_side_effects=True, vmem_limit_bytes=40 << 20
        ),
    )(*operands)


def solution(mesh):
    in_specs = (
        P(("blk", "rep"), None, None, None),
        P(("blk", "rep"), None),
        P(("blk", "rep")),
        P(("blk", "rep"), None),
    )
    out_specs = P(("blk", "rep"), None, None, None)
    return jax.shard_map(
        on_device, mesh=mesh, in_specs=in_specs, out_specs=out_specs, check_vma=False
    )
```

```python
import jax
import jax.numpy as jnp
from jax import lax
from jax.experimental import pallas as pl
from jax.experimental.pallas import tpu as pltpu
from jax.sharding import PartitionSpec as P

B = 128
LIST = 4
W = 3
ITERS = 5
BAND = 7
ROWS = 4
EXT = ROWS + 2 * W
F32 = jnp.float32
BF16 = jnp.bfloat16
MESH = pl.DeviceIdType.MESH


def terms(row, col):
    low, high = min(row, col), max(row, col)
    return [z for z in range(ROWS) if z <= low and high <= z + 2 * W]


FAR = [(r, c) for r in range(W) for c in range(r + W + 1)]
NEAR = [(9 - r, 9 - c) for r, c in FAR]
FAR_SENDS = [[t for t in FAR if max(terms(*t)) == z] for z in range(W)]
NEAR_SENDS = [
    [t for t in NEAR if terms(*t) == [ROWS - 1]],
    [t for t in NEAR if terms(*t) != [ROWS - 1]],
]
FAR_SENDS[0] = [(0, 0), (0, 3), (0, 1), (0, 2)]
SHARED = [(0, 1), (0, 2)]
STARTS = [0, 4, 9]
FAR_BLOCKS = 13
MIRRORED = [(a, b) for a in range(LIST // 2, LIST) for b in range(LIST // 2)]
EARLY = 3


def kernel(
    lists_hbm, weights_hbm, scales_hbm, ham, owned, lists, weights, scales, window, sym, xs, ys, qs, result,
    far_out, far_line_out, near_out, far_in, far_line_in, near_in,
    ready, small_sem, load_sem, halo_send, halo_recv, far_send, far_recv, near_send, near_recv,
):
    chip = lax.axis_index("blk")
    core = lax.axis_index("rep")
    chips = lax.axis_size("blk")
    total = ROWS * 2 * chips
    first = (chip * 2 + core) * ROWS
    near = (chip, 1 - core)
    far = (lax.rem(chip + 2 * core - 1 + chips, chips), 1 - core)

    def mirrored(value, last):
        return value + core * (last - 2 * value)

    barrier = pltpu.get_barrier_semaphore()
    for device in (far, near):
        pl.semaphore_signal(barrier, inc=1, device_id=device, device_id_type=MESH)
    small = [
        pltpu.make_async_copy(source, target, small_sem.at[i])
        for i, (source, target) in enumerate(
            ((lists_hbm, lists), (weights_hbm, weights), (scales_hbm, scales))
        )
    ]
    for copy in small:
        copy.start()
    load = pltpu.make_async_copy(ham, window.at[pl.ds(W, ROWS)], load_sem)
    load.start()
    for copy in small:
        copy.wait()

    position, place, share, member = [], [], [], []
    for z in range(ROWS):
        j = mirrored(z, ROWS - 1)
        spots = []
        for a in range(LIST):
            e = jnp.clip(lax.rem(lists[j, a] - first + W + total, total), 0, EXT - 1)
            spots.append(mirrored(e, EXT - 1))
        position.append(spots)
        places, shares, members = [], [], []
        for u in range(2 * W + 1):
            where = jnp.int32(0)
            weight = jnp.float32(0.0)
            here = jnp.float32(0.0)
            for a in range(LIST):
                hit = spots[a] == z + u
                where = jnp.where(hit, jnp.int32(a), where)
                weight = jnp.where(hit, weights[j, a], weight)
                here = jnp.where(hit, jnp.float32(1.0), here)
            places.append(where)
            shares.append(weight)
            members.append(here)
        place.append(places)
        share.append(shares)
        member.append(members)

    @pl.when(core == 1)
    def _():
        pl.semaphore_wait(barrier, 2)
        pl.semaphore_signal(ready, inc=1, device_id=near, device_id_type=MESH)

    @pl.when(core == 0)
    def _():
        pl.semaphore_wait(ready, 1)

    far_runs = [[(2, 3, 4)], [(1, 3, 4), (2, 2, 1)], [(0, 3, 4), (1, 2, 1), (2, 1, 1)]]
    near_runs = [[(7, 0, 6), (8, 0, 5), (9, 0, 4)]]

    def halo(runs, device, corner, index):
        copies, arrivals = [], []
        for y, slot, count in runs:
            flipped = BAND - slot - count
            low = core * slot + (1 - core) * flipped
            low_here = (1 - core) * slot + core * flipped
            row = mirrored(corner - y, EXT - 1) - W
            there = core * y + (1 - core) * (EXT - 1 - y)
            for dst, source, kept in ((there, low, copies), (mirrored(y, EXT - 1), low_here, arrivals)):
                kept.append(pltpu.make_async_remote_copy(
                    src_ref=ham.at[row, pl.ds(source, count)],
                    dst_ref=window.at[dst, pl.ds(source, count)],
                    send_sem=halo_send.at[index],
                    recv_sem=halo_recv.at[index],
                    device_id=device,
                    device_id_type=MESH,
                ))
            index += 1
        return copies, arrivals

    near_copies, near_arrivals = halo(near_runs[0], near, 13, 0)
    far_copies, far_arrivals = [], []
    index = 3
    for runs in far_runs:
        copies, arrivals = halo(runs, far, 5, index)
        far_copies.append(copies)
        far_arrivals.append(arrivals)
        index += len(runs)
    @pl.when(core == 1)
    def _():
        for copy in sum(far_copies, []) + near_copies:
            copy.start()

    @pl.when(core == 0)
    def _():
        for copy in near_copies:
            copy.start()
        pl.semaphore_wait(barrier, 2)
        for copy in sum(far_copies, []):
            copy.start()


    def symmetrize(low, o):
        high = low + o
        slot = W + o * (1 - 2 * core)
        upper = window[mirrored(low, EXT - 1), slot]
        lower = window[mirrored(high, EXT - 1), 2 * W - slot]
        both = 0.5 * (upper.astype(F32) + lower.T.astype(F32))
        sym[low, W + o] = both
        if o:
            sym[high, W - o] = 0.5 * (lower.astype(F32) + upper.T.astype(F32))

    load.wait()
    for o in range(W + 1):
        for low in range(W, W + ROWS - o):
            symmetrize(low, o)
    for arrival in near_arrivals:
        arrival.wait_recv()
    for o in range(W + 1):
        for high in range(W + ROWS, EXT):
            symmetrize(high - o, o)

    on_diagonal = (
        lax.broadcasted_iota(jnp.int32, (B, B), 0) == lax.broadcasted_iota(jnp.int32, (B, B), 1)
    )
    diagonal = on_diagonal.astype(F32)
    size, half = LIST * B, LIST * B // 2

    def assemble(z):
        spots = position[z]
        scale = scales[mirrored(z, ROWS - 1)]
        for a in range(LIST):
            for b in range(LIST):
                offset = spots[b] - spots[a]
                stored = jnp.where(jnp.abs(offset) <= W, scale, jnp.float32(0.0))
                slot = jnp.clip(offset + W, 0, BAND - 1)
                block = stored * sym[spots[a], slot]
                if (a, b) not in MIRRORED:
                    xs[z, a * B : a * B + B, b * B : b * B + B] = block
                ys[z, 0, a * B : a * B + B, b * B : b * B + B] = block.astype(BF16)

    low, high, whole = slice(0, half), slice(half, size), slice(0, size)
    quarters = ((low, high), (high, high), (low, low))

    def iterate(z, steps):
        base = z * LIST * LIST
        for k in steps:
            now, later = k % 2, (k + 1) % 2
            for rows, cols in (quarters[1], quarters[0], quarters[2]):
                square = jnp.dot(
                    ys[z, now, rows, whole], ys[z, now, whole, cols], preferred_element_type=F32
                ).astype(BF16)
                qs[z, now, rows, cols] = square
                if rows != cols:
                    qs[z, now, cols, rows] = square.T
            for rows, cols in quarters:
                value = 1.5 * xs[z, rows, cols] - 0.5 * jnp.dot(
                    ys[z, now, rows, whole], qs[z, now, whole, cols], preferred_element_type=F32
                )
                if k < ITERS - 1:
                    xs[z, rows, cols] = value
                    rounded = value.astype(BF16)
                    ys[z, later, rows, cols] = rounded
                    if rows != cols:
                        ys[z, later, cols, rows] = rounded.T
                    continue
                for m in range(LIST // 2):
                    for n in range(LIST // 2):
                        a, b = rows.start // B + m, cols.start // B + n
                        block = value[m * B : m * B + B, n * B : n * B + B]
                        block = 0.5 * (diagonal - block) if a == b else -0.5 * block
                        result[base + a * LIST + b] = block
                        if rows != cols:
                            result[base + b * LIST + a] = block.T

    def gathered(row, col):
        value = None
        for z in terms(row, col):
            u, v = row - z, col - z
            factor = share[z][u] * member[z][v]
            term = factor * result[z * LIST * LIST + place[z][u] * LIST + place[z][v]]
            value = term if value is None else value + term
        return value

    def far_contributions(z):
        ends = [0, 2, 4] if z == 0 else [0, len(FAR_SENDS[z])]
        runs = [pl.ds(STARTS[z] + low, high - low) for low, high in zip(ends, ends[1:])]
        return [
            pltpu.make_async_remote_copy(
                src_ref=source,
                dst_ref=target,
                send_sem=far_send.at[z, i],
                recv_sem=far_recv.at[z, i],
                device_id=far,
                device_id_type=MESH,
            )
            for i, (source, target) in enumerate(
                [(far_line_out.at[z], far_line_in.at[z])]
                + [(far_out.at[run], far_in.at[run]) for run in runs]
            )
        ]

    def near_contribution(i):
        low, count = i * len(NEAR_SENDS[0]), len(NEAR_SENDS[i])
        return pltpu.make_async_remote_copy(
            src_ref=near_out.at[pl.ds(low, count)],
            dst_ref=near_in.at[pl.ds(low, count)],
            send_sem=near_send.at[i],
            recv_sem=near_recv.at[i],
            device_id=near,
            device_id_type=MESH,
        )

    def send_far(z):
        copies = far_contributions(z)
        for i, target in enumerate(FAR_SENDS[z]):
            if target in SHARED:
                u, v = target
                factor = member[z][u] * member[z][v]
                block = factor * result[z * LIST * LIST + place[z][u] * LIST + place[z][v]]
            else:
                block = gathered(*target)
            if target == (z, z):
                line = jnp.sum(jnp.where(on_diagonal, block, 0.0), axis=0, keepdims=True)
                lines = jnp.broadcast_to(line, (8, B))
                if z == 0:
                    row = lax.broadcasted_iota(jnp.int32, (8, B), 0)
                    for u in range(W):
                        lines = jnp.where(row == u + 1, share[z][u], lines)
                far_line_out[z] = lines
                block = jnp.where(on_diagonal, 0.0, block)
            far_out[STARTS[z] + i] = block.astype(BF16)
            if z == 0 and i == 1:
                copies[1].start()
        copies[-1].start()
        copies[0].start()

    def send_near(i):
        for n, target in enumerate(NEAR_SENDS[i]):
            near_out[i * len(NEAR_SENDS[0]) + n] = gathered(*target)
        near_contribution(i).start()

    def far_halo(group):
        low = W - 1 - group
        for arrival in far_arrivals[group]:
            arrival.wait_recv()
        for o in range(W + 1):
            symmetrize(low, o)

    last = ROWS - 1
    assemble(last)
    iterate(last, range(ITERS))
    far_halo(0)
    assemble(2)
    iterate(2, range(EARLY))
    far_halo(1)
    assemble(1)
    iterate(1, range(3))
    far_halo(2)
    assemble(0)
    iterate(0, range(ITERS))
    send_far(0)
    iterate(1, range(3, ITERS))
    send_far(1)
    iterate(2, range(EARLY, ITERS))
    send_far(2)
    send_near(1)
    send_near(0)

    def spot(row, col):
        return mirrored(row - W, ROWS - 1), mirrored(col - row + W, BAND - 1)

    for row in range(W, W + ROWS):
        for col in range(row - W, row + W + 1):
            r, s = spot(row, col)
            owned[r, s] = gathered(row, col)

    def add_far(z):
        for copy in far_contributions(z):
            copy.wait_recv()
        for i, (row, col) in enumerate(FAR_SENDS[z]):
            block = far_in[STARTS[z] + i].astype(F32)
            if (row, col) in SHARED:
                r, s = spot(5 - col, 5 - row)
                owned[r, s] += far_line_in[z, 1 + col : 2 + col, :] * block.T
                block = far_line_in[z, 1 + row : 2 + row, :] * block
            if row == col:
                block = jnp.where(on_diagonal, far_line_in[z, 0:1, :], block)
            r, s = spot(5 - row, 5 - col)
            owned[r, s] += block

    def add_near(i):
        near_contribution(i).wait_recv()
        for n, (row, col) in enumerate(NEAR_SENDS[i]):
            r, s = spot(13 - row, 13 - col)
            owned[r, s] += near_in[i * len(NEAR_SENDS[0]) + n]

    add_far(0)
    add_far(1)
    add_near(1)
    add_near(0)
    add_far(2)
    for copy in near_copies + sum(far_copies, []):
        copy.wait_send()
    for z in range(W):
        for copy in far_contributions(z):
            copy.wait_send()
    for i in range(2):
        near_contribution(i).wait_send()


def on_device(hamiltonian, lists, scales, weights):
    hbm = pl.BlockSpec(memory_space=pl.ANY)
    operands = [
        pltpu.with_memory_space_constraint(value, pltpu.HBM)
        for value in (lists, weights, scales, hamiltonian)
    ]
    size = LIST * B
    return pl.pallas_call(
        kernel,
        name="density",
        out_shape=jax.ShapeDtypeStruct((ROWS, BAND, B, B), F32),
        in_specs=[hbm] * 4,
        out_specs=pl.BlockSpec(memory_space=pltpu.VMEM),
        scratch_shapes=[
            pltpu.SMEM((ROWS, LIST), jnp.int32),
            pltpu.SMEM((ROWS, LIST), F32),
            pltpu.SMEM((ROWS,), F32),
            pltpu.VMEM((EXT, BAND, B, B), BF16),
            pltpu.VMEM((EXT, BAND, B, B), F32),
            pltpu.VMEM((ROWS, size, size), F32),
            pltpu.VMEM((ROWS, 2, size, size), BF16),
            pltpu.VMEM((ROWS, 2, size, size), BF16),
            pltpu.VMEM((ROWS * LIST * LIST, B, B), F32),
            pltpu.VMEM((FAR_BLOCKS, B, B), BF16),
            pltpu.VMEM((W, 8, B), F32),
            pltpu.VMEM((len(NEAR), B, B), F32),
            pltpu.VMEM((FAR_BLOCKS, B, B), BF16),
            pltpu.VMEM((W, 8, B), F32),
            pltpu.VMEM((len(NEAR), B, B), F32),
            pltpu.SemaphoreType.REGULAR,
            pltpu.SemaphoreType.DMA((3,)),
            pltpu.SemaphoreType.DMA,
            pltpu.SemaphoreType.DMA((9,)),
            pltpu.SemaphoreType.DMA((9,)),
            pltpu.SemaphoreType.DMA((W, W)),
            pltpu.SemaphoreType.DMA((W, W)),
            pltpu.SemaphoreType.DMA((2,)),
            pltpu.SemaphoreType.DMA((2,)),
        ],
        compiler_params=pltpu.CompilerParams(
            collective_id=0, has_side_effects=True, vmem_limit_bytes=40 << 20
        ),
    )(*operands)


def solution(mesh):
    in_specs = (
        P(("blk", "rep"), None, None, None),
        P(("blk", "rep"), None),
        P(("blk", "rep")),
        P(("blk", "rep"), None),
    )
    out_specs = P(("blk", "rep"), None, None, None)
    return jax.shard_map(
        on_device, mesh=mesh, in_specs=in_specs, out_specs=out_specs, check_vma=False
    )
```
